512 devices in a mesh: region: 8 (over z_hi, x), blk: 64 (over y, z_lo, core).
Axes of the slice: x: 4, y: 4, z: 16 (z_hi: 2, z_lo: 8; z = z_hi * 8 + z_lo), core: 2. Of those that a mesh axis runs over, the one named last changes fastest.
Arguments:
- records: float32 [2048, 2048], P(('region', 'blk')), may hold values from -6 to 6
- starts: int32 [2048], P(('region', 'blk')), may hold values from 0 to 1024
- tapers: int32 [2048], P(('region', 'blk')), may hold values from 2 to 256
- pair_a: int32 [393216], P(('region', 'blk')), may hold values from 0 to 3
- pair_b: int32 [393216], P(('region', 'blk')), may hold values from 0 to 255
- pair_count: int32 [512], P(('region', 'blk')), may hold values from 192 to 768, as said below
- observed: float32 [393216, 512], P(('region', 'blk')), may hold values from -6 to 6
Outputs:
- correlations: float32 [393216, 512], P(('region', 'blk'))
- far_correlations: float32 [2048, 512], P(('region', 'blk'))
- adjoint: float32 [2048, 1024], P(('region', 'blk'))
The draws below stay inside these ranges and needn't reach their ends.
Inputs may be any that keep to these rules, and one draw needn't show every extreme that they name: `pair_count`: device 0 has all 768 slots live.
All inputs are finite; a program needn't handle non-finite values.
Results may differ from the reference program's by a relative error of at most 0.0003.
Values sent between devices are 32-bit elements; how exact they have to be, the bound alone decides.
A program may use at most 64 MiB of HBM per device.

```python
import math
import jax
import jax.numpy as jnp
from jax import lax

S_DEV = 4
REC = 2048
WIN = 1024
P_DEV = 768
NF = 512
LAGS = 512
S_GRP = 256
STATIONS = 2048
PAIRS = 393216
N_BLK = 64
DEVICES = 512


def draw_pair_count(key, part):
    counts = jax.random.randint(key, (DEVICES,), P_DEV // 4, P_DEV + 1)
    first = jnp.arange(DEVICES, dtype=jnp.int32) == 0
    return jnp.where(first, P_DEV, counts).astype(jnp.int32)


def with_ends(array, own_key, low, high):
    longest = array.shape.index(max(array.shape))
    spots = []
    for shift in (0, 1):
        where = [jax.random.randint(jax.random.fold_in(own_key, axis), (), 0, length) for axis, length in enumerate(array.shape)]
        where[longest] = (where[longest] + shift) % array.shape[longest]
        spots.append(tuple(where))
    return array.at[spots[0]].set(low).at[spots[1]].set(high)


def block_scale(key, extent, cuts, least, largest):
    gain, own = 1.0, jax.random.fold_in(key, 6)
    for dim, parts in cuts:
        heights = jnp.exp(jax.random.uniform(jax.random.fold_in(own, dim), (parts,), jnp.float32, least / len(cuts), largest / len(cuts)))
        gain = gain * jnp.repeat(heights, extent[dim] // parts).reshape([-1 if axis == dim else 1 for axis in range(len(extent))])
    return gain


def scatter_about(stream_key, shape, width, limit, pieces=(), held_as=jnp.bfloat16):
    drawn = jax.random.normal(stream_key, shape, jnp.float32) * width
    if len(pieces) > 0:
        drawn = block_scale(stream_key, shape, pieces, -0.22, 0.18) * drawn
    return jnp.clip(drawn, min=-limit, max=limit).astype(held_as)


def setup_inputs(seed: int = 0) -> dict:
    seeds = jax.random.split(jax.random.key(seed), 8)
    return {
        "records": scatter_about(seeds[0], (STATIONS, REC), 1.0, 6.0, ((0, 512),), jnp.float32),
        "starts": with_ends(jax.random.randint(seeds[1], (STATIONS,), 0, REC - WIN + 1), jax.random.fold_in(seeds[1], 1), 0, REC - WIN).astype(jnp.int32),
        "tapers": with_ends(jax.random.randint(seeds[2], (STATIONS,), 2, WIN // 4 + 1), jax.random.fold_in(seeds[2], 1), 2, (WIN // 4 + 1) - 1).astype(jnp.int32),
        "pair_a": with_ends(jax.random.randint(seeds[3], (PAIRS,), 0, S_DEV), jax.random.fold_in(seeds[3], 1), 0, S_DEV - 1).astype(jnp.int32),
        "pair_b": with_ends(jax.random.randint(seeds[4], (PAIRS,), 0, S_GRP), jax.random.fold_in(seeds[4], 1), 0, S_GRP - 1).astype(jnp.int32),
        "pair_count": draw_pair_count(jax.random.fold_in(seeds[7], 71), 0),
        "observed": scatter_about(seeds[6], (PAIRS, LAGS), 1.0, 6.0, ((0, 512),), jnp.float32),
    }


def phase_table(rows, cols, length):
    product = (rows[:, None] * cols[None, :]) % length
    return product.astype(jnp.float32) * (2.0 * math.pi / length)


def taper_windows(records, starts, tapers):
    sample = jnp.arange(WIN, dtype=jnp.int32)
    picked = jnp.take_along_axis(records, starts[:, None] + sample[None, :], axis=1)
    lengths = tapers.astype(jnp.float32)[:, None]
    position = sample.astype(jnp.float32)[None, :]
    shape_fn = jnp.minimum(1.0, jnp.minimum((position + 1.0) / lengths, (WIN - position) / lengths))
    return picked * shape_fn * (WIN ** -0.25)


def to_spectra(windows):
    angle = phase_table(jnp.arange(WIN, dtype=jnp.int32), jnp.arange(NF, dtype=jnp.int32), WIN)
    real_part = jnp.dot(windows, jnp.cos(angle), precision=lax.Precision.HIGHEST)
    imag_part = jnp.dot(windows, -jnp.sin(angle), precision=lax.Precision.HIGHEST)
    return jnp.concatenate([real_part, imag_part], axis=1)


def bin_weights():
    bins = jnp.arange(NF, dtype=jnp.int32)
    weight = jnp.where(bins == 0, 1.0, 2.0).astype(jnp.float32) / WIN
    return jnp.concatenate([weight, weight])


def lag_index():
    return (jnp.arange(LAGS, dtype=jnp.int32) - LAGS // 2) % WIN


def to_lags(cross_spec):
    angle = phase_table(jnp.arange(NF, dtype=jnp.int32), lag_index(), WIN)
    table = jnp.concatenate([jnp.cos(angle), -jnp.sin(angle)], axis=0)
    return jnp.dot(cross_spec * bin_weights()[None, :], table, precision=lax.Precision.HIGHEST)


def from_lags(residual):
    angle = phase_table(lag_index(), jnp.arange(NF, dtype=jnp.int32), WIN)
    table = jnp.concatenate([jnp.cos(angle), -jnp.sin(angle)], axis=1)
    return jnp.dot(residual, table, precision=lax.Precision.HIGHEST)


def to_time(source):
    angle = phase_table(jnp.arange(NF, dtype=jnp.int32), jnp.arange(WIN, dtype=jnp.int32), WIN)
    weighted = source * bin_weights()[None, :]
    first = jnp.dot(weighted[:, :NF], jnp.cos(angle), precision=lax.Precision.HIGHEST)
    second = jnp.dot(weighted[:, NF:], jnp.sin(angle), precision=lax.Precision.HIGHEST)
    return (first - second) * (1.0 / 16.0)


def cross(left, right):
    left_r, left_i = left[:, :NF], left[:, NF:]
    right_r, right_i = right[:, :NF], right[:, NF:]
    return jnp.concatenate([left_r * right_r + left_i * right_i, left_i * right_r - left_r * right_i], axis=1)


def times_plain(misfit, spec):
    mis_r, mis_i = misfit[:, :NF], misfit[:, NF:]
    spec_r, spec_i = spec[:, :NF], spec[:, NF:]
    return jnp.concatenate([mis_r * spec_r - mis_i * spec_i, mis_r * spec_i + mis_i * spec_r], axis=1)


def times_conj(misfit, spec):
    mis_r, mis_i = misfit[:, :NF], misfit[:, NF:]
    spec_r, spec_i = spec[:, :NF], spec[:, NF:]
    return jnp.concatenate([mis_r * spec_r + mis_i * spec_i, mis_r * spec_i - mis_i * spec_r], axis=1)


def reference(records, starts, tapers, pair_a, pair_b, pair_count, observed):
    spectra = to_spectra(taper_windows(records, starts, tapers))
    prior = jnp.roll(spectra, S_GRP, axis=0)
    far_correlations = to_lags(cross(spectra, prior))

    def device_step(summed, device):
        first = lax.dynamic_slice_in_dim(pair_a, device * P_DEV, P_DEV)
        second = lax.dynamic_slice_in_dim(pair_b, device * P_DEV, P_DEV)
        seen = lax.dynamic_slice_in_dim(observed, device * P_DEV, P_DEV, 0)
        group = device // N_BLK
        own_rows = (device * S_DEV + first).astype(jnp.int32)
        far_rows = (group * S_GRP + second).astype(jnp.int32)
        source_spec = jnp.take(spectra, own_rows, axis=0)
        target_spec = jnp.take(spectra, far_rows, axis=0)
        count = pair_count[device]
        live_rows = (jnp.arange(P_DEV, dtype=jnp.int32) < count).astype(jnp.float32)[:, None]
        corr_raw = to_lags(cross(source_spec, target_spec))
        misfit = from_lags((corr_raw - seen) * live_rows)
        summed = summed.at[own_rows].add(times_plain(misfit, target_spec))
        summed = summed.at[far_rows].add(times_conj(misfit, source_spec))
        return summed, corr_raw * live_rows

    start_sum = jnp.zeros((STATIONS, 2 * NF), jnp.float32)
    summed, blocks = lax.scan(device_step, start_sum, jnp.arange(DEVICES, dtype=jnp.int32))
    correlations = blocks.reshape(PAIRS, LAGS)
    adjoint = to_time(summed)
    return correlations, far_correlations, adjoint
```

```python
import jax
import jax.numpy as jnp
import ml_dtypes
import numpy as np
from jax import lax
from jax.experimental import pallas as pl
from jax.experimental.pallas import tpu as pltpu
from jax.sharding import PartitionSpec as P

WIN = 1024
HALF = 512
QUARTER = 256
TILE = 128
LANES = 128
F32 = jnp.float32
BF16 = jnp.bfloat16
MESH = pl.DeviceIdType.MESH
NY, NZ = 4, 8


def tables():
    t = np.arange(HALF)[:, None]
    parts = []
    for parity in (0, 1):
        k = 2 * np.arange(QUARTER)[None, :] + parity
        angle = 2.0 * np.pi * ((t * k) % WIN) / WIN
        full = np.concatenate([np.cos(angle), -np.sin(angle)], axis=1)
        high = full.astype(ml_dtypes.bfloat16)
        low = (full - high.astype(np.float64)).astype(ml_dtypes.bfloat16)
        parts += [high, low]
    return np.stack(parts)


def split(x):
    high = x.astype(BF16)
    return high, (x - high.astype(F32)).astype(BF16)


def dot_nn(a, b):
    return lax.dot_general(a, b, (((1,), (0,)), ((), ())), preferred_element_type=F32)


def dot_nt(a, b):
    return lax.dot_general(a, b, (((1,), (1,)), ((), ())), preferred_element_type=F32)


def dot3(dot, pair, high, low):
    return dot(pair[0], high) + dot(pair[1], high) + dot(pair[0], low)


def place():
    blk = lax.axis_index("blk")
    core = blk % 2
    z = (blk // 2) % NZ
    y = blk // (2 * NZ)
    sign = 1 - 2 * core
    return {
        "core": core,
        "z": z,
        "y": y,
        "up": (y + sign + NY) % NY,
        "down": (y - sign + NY) % NY,
        "across": (y + 2) % NY,
    }


def flip(z, d):
    out = 0
    for bit in (1, 2, 4):
        own = (z // bit) % 2
        out = out + bit * ((own + (d // bit) % 2) % 2)
    return out


def device(y, z, core):
    return y * (2 * NZ) + z * 2 + core


def slot_of(core, y, z):
    return (core * NY + y) * NZ + z


def enter(at):
    y, z, core = at["y"], at["z"], at["core"]
    peers = [device(y, z, 1 - core), device(at["up"], z, core), device(at["down"], z, core)]
    peers += [device(y, flip(z, d), core) for d in (1, 2, 3, 4)]
    barrier = pltpu.get_barrier_semaphore()
    for peer in peers:
        pl.semaphore_signal(barrier, inc=1, device_id={"blk": peer}, device_id_type=MESH)
    return barrier, len(peers)


def window_tiles(records, starts, tapers, stage):
    lane = lax.broadcasted_iota(jnp.int32, (8, LANES), 1)
    sample = lax.broadcasted_iota(jnp.int32, (8, LANES), 0) * LANES + lane
    position = sample.astype(F32)
    tiles = []
    for i in range(4):
        base = i * 16
        for c in range(16):
            stage[base + c : base + c + 1, :] = records[i : i + 1, c * LANES : (c + 1) * LANES]
        chunks = stage[base : base + 16, :]
        start = jnp.full((16, LANES), starts[i], jnp.int32)
        for bit in (1, 2, 4, 8):
            chunks = jnp.where(start & (bit * LANES) != 0, pltpu.roll(chunks, 16 - bit, 0), chunks)
        first, second = chunks[0:8, :], pltpu.roll(chunks, 15, 0)[0:8, :]
        start = start[0:8, :]
        for bit in (1, 2, 4, 8, 16, 32, 64):
            moved_first = pltpu.roll(first, LANES - bit, 1)
            moved_second = pltpu.roll(second, LANES - bit, 1)
            taken = start & bit != 0
            first = jnp.where(taken, jnp.where(lane < LANES - bit, moved_first, moved_second), first)
            second = jnp.where(taken, moved_second, second)
        length = jnp.full((8, LANES), tapers[i], jnp.int32).astype(F32)
        shape_fn = jnp.minimum(1.0, jnp.minimum((position + 1.0) / length, (WIN - position) / length))
        tiles.append(first * shape_fn * WIN ** (-0.25))
    return tiles


class Sender:
    def __init__(self, sems):
        self.sems, self.count, self.sent = sems, 0, []

    def __call__(self, src, dst, recv, target):
        copy = pltpu.make_async_remote_copy(
            src_ref=src,
            dst_ref=dst,
            send_sem=self.sems.at[self.count],
            recv_sem=recv,
            device_id=target,
            device_id_type=MESH,
        )
        copy.start()
        self.count += 1
        self.sent.append(copy)

    def drain(self):
        for copy in self.sent:
            copy.wait_send()


def arrived(dst, recv, sems, at):
    pltpu.make_async_remote_copy(
        src_ref=dst,
        dst_ref=dst,
        send_sem=sems.at[0],
        recv_sem=recv,
        device_id={"blk": device(at["y"], at["z"], 1 - at["core"])},
        device_id_type=MESH,
    ).wait_recv()


def gather_kernel(starts, tapers, records, group, near, stage, send_sems, recv_sems, far_sem):
    at = place()
    y, z, core = at["y"], at["z"], at["core"]
    region = lax.axis_index("region")
    regions = lax.axis_size("region")
    after, before = lax.rem(region + 1, regions), lax.rem(region + regions - 1, regions)
    barrier, count = enter(at)
    for other in (after, before):
        pl.semaphore_signal(barrier, inc=1, device_id={"region": other}, device_id_type=MESH)
    tiles = window_tiles(records, starts, tapers, stage)
    mine = slot_of(core, y, z)
    for i in range(4):
        group[pl.ds(pl.multiple_of(mine * 32, 32) + i * 8, 8), :] = tiles[i]
        near[i * 8 : i * 8 + 8, :] = tiles[i]
    pl.semaphore_wait(barrier, count + 2)

    send = Sender(send_sems)

    def rows(slot):
        return group.at[pl.ds(pl.multiple_of(slot * 32, 32), 32), :]

    def pass_on(slot, yy, zz, cc):
        send(rows(slot), rows(slot), recv_sems.at[slot], {"blk": device(yy, zz, cc)})

    def take(slot):
        arrived(rows(slot), recv_sems.at[slot], send_sems, at)

    def column(d):
        slot = slot_of(core, y, flip(z, d))
        if d:
            take(slot)
        if d == 0:
            for e in (4, 1, 2, 3):
                pass_on(slot, y, flip(z, e), core)
        if d == 4:
            for e in (1, 2, 3):
                pass_on(slot, y, flip(z, e), core)
        pass_on(slot, at["up"], z, core)
        pass_on(slot, at["down"], z, core)
        pass_on(slot, y, z, 1 - core)

    def beside(d):
        zz = flip(z, d)
        slot = slot_of(core, at["down"], zz)
        take(slot)
        pass_on(slot, at["up"], z, core)
        pass_on(slot, y, z, 1 - core)
        slot = slot_of(core, at["up"], zz)
        take(slot)
        pass_on(slot, y, z, 1 - core)

    def opposite(d):
        slot = slot_of(core, at["across"], flip(z, d))
        take(slot)
        pass_on(slot, y, z, 1 - core)

    column(0)
    send(near.at[0:32, :], near.at[32:64, :], far_sem.at[0], {"region": after})
    near_by, next_to, far_side = column, beside, opposite
    for step, d in (
        (near_by, 1), (next_to, 0), (near_by, 2), (near_by, 3), (next_to, 1), (far_side, 0), (near_by, 4),
        (next_to, 2), (far_side, 1), (next_to, 3), (far_side, 2), (next_to, 4), (near_by, 5), (far_side, 3),
        (near_by, 6), (near_by, 7), (next_to, 5), (far_side, 4), (next_to, 6), (next_to, 7), (far_side, 5),
        (far_side, 6), (far_side, 7),
    ):
        step(d)
    for yy in range(NY):
        for zz in range(NZ):
            take(slot_of(1 - core, yy, zz))
    arrived(near.at[32:64, :], far_sem.at[0], send_sems, at)
    send.drain()


def complex_parts(x):
    return x[:, :QUARTER], x[:, QUARTER:HALF], x[:, HALF : HALF + QUARTER], x[:, HALF + QUARTER :]


def spectra_of(tile_of, table):
    pieces = [tile_of(c) for c in range(8)]
    early = jnp.concatenate(pieces[:4], axis=1)
    late = jnp.concatenate(pieces[4:], axis=1)
    even = dot3(dot_nn, split(early + late), table[0], table[1])
    odd = dot3(dot_nn, split(early - late), table[2], table[3])
    return jnp.concatenate([even, odd], axis=1)


def cross(left, right):
    lr, li, mr, mi = complex_parts(left)
    rr, ri, sr, si = complex_parts(right)
    even = jnp.concatenate([lr * rr + li * ri, li * rr - lr * ri], axis=1)
    odd = jnp.concatenate([mr * sr + mi * si, mi * sr - mr * si], axis=1)
    return even, odd


def halve_first(x):
    lane = lax.broadcasted_iota(jnp.int32, (1, HALF), 1)
    return x * jnp.where(lane == 0, 0.5, 1.0).astype(F32)


def spread(row):
    return jnp.broadcast_to(row, (LANES, LANES)).T


def pairs_kernel(
    count, group, near, pair_a, pair_b, observed, table, corr, remote, local, far, spec, own, conj_terms, plain_terms
):
    slots = corr.shape[0]
    spectra = spectra_of(lambda c: group[pl.ds(c, QUARTER, stride=8), :], table)
    high, low = split(spectra)
    spec[0:QUARTER, :] = high
    spec[QUARTER:HALF, :] = low
    ends = spectra_of(lambda c: near[pl.ds(c, 8, stride=8), :], table)
    own[...] = ends
    far_even, far_odd = cross(ends[0:4, :], ends[4:8, :])
    far[...] = jnp.concatenate([halve_first(far_even), far_odd], axis=1)
    live_count = count[0]
    lane = lax.broadcasted_iota(jnp.int32, (TILE, LANES), 1)

    def tile(i, carry):
        rows = pl.ds(pl.multiple_of(i * TILE, TILE), TILE)
        low_rows = pl.ds(pl.multiple_of(slots + i * TILE, TILE), TILE)
        b_col = spread(pair_b[pl.ds(i, 1), :])
        a_col = spread(pair_a[pl.ds(i, 1), :])
        hot = jnp.concatenate([b_col == lane, b_col == lane + LANES], axis=1).astype(F32).astype(BF16)
        target = dot_nn(hot, spec[0:QUARTER, :]) + dot_nn(hot, spec[QUARTER:HALF, :])
        pieces = []
        for c in range(8):
            cut = slice(c * LANES, (c + 1) * LANES)
            row = [jnp.broadcast_to(own[q : q + 1, cut], (TILE, LANES)) for q in range(4)]
            pieces.append(
                jnp.where(a_col == 0, row[0], jnp.where(a_col == 1, row[1], jnp.where(a_col == 2, row[2], row[3])))
            )
        source = jnp.concatenate(pieces, axis=1)
        even, odd = cross(source, target)
        lag_even = dot3(dot_nt, split(halve_first(even)), table[0], table[1])
        lag_odd = dot3(dot_nt, split(odd), table[2], table[3])
        ahead = (lag_even[:, :QUARTER] + lag_odd[:, :QUARTER]) * (2.0 / WIN)
        behind = (lag_even[:, QUARTER:] - lag_odd[:, QUARTER:]) * (2.0 / WIN)
        number = lax.broadcasted_iota(jnp.int32, (TILE, QUARTER), 0) + i * TILE
        live = number < live_count
        corr[rows, 0:QUARTER] = jnp.where(live, behind, 0.0)
        corr[rows, QUARTER:HALF] = jnp.where(live, ahead, 0.0)
        res_behind = split(jnp.where(live, behind - observed[rows, 0:QUARTER], 0.0))
        res_ahead = split(jnp.where(live, ahead - observed[rows, QUARTER:HALF], 0.0))
        plus = [jnp.concatenate([res_ahead[q], res_behind[q]], axis=1) for q in (0, 1)]
        minus = [jnp.concatenate([res_ahead[q], -res_behind[q]], axis=1) for q in (0, 1)]
        mis_even = dot3(dot_nn, plus, table[0], table[1])
        mis_odd = dot3(dot_nn, minus, table[2], table[3])
        for p, mis in ((0, mis_even), (1, mis_odd)):
            mr, mi = mis[:, :QUARTER], mis[:, QUARTER:]
            base = p * HALF
            sr, si = source[:, base : base + QUARTER], source[:, base + QUARTER : base + HALF]
            tr, ti = target[:, base : base + QUARTER], target[:, base + QUARTER : base + HALF]
            for terms, re, im in (
                (conj_terms, mr * sr + mi * si, mr * si - mi * sr),
                (plain_terms, mr * tr - mi * ti, mr * ti + mi * tr),
            ):
                for offset, part in ((0, re), (QUARTER, im)):
                    part_high, part_low = split(part)
                    cut = slice(base + offset, base + offset + QUARTER)
                    terms[rows, cut] = part_high
                    terms[low_rows, cut] = part_low
        return carry

    lax.fori_loop(0, slots // TILE, tile, 0)

    def hot_rows(index, height):
        down = lax.broadcasted_iota(jnp.int32, (height, LANES), 0)
        cols = [
            (jnp.broadcast_to(index[i : i + 1, :], (height, LANES)) == down).astype(F32).astype(BF16)
            for i in range(slots // LANES)
        ]
        return jnp.concatenate(cols + cols, axis=1)

    totals = dot_nn(hot_rows(pair_b, QUARTER), conj_terms[...])
    own_totals = dot_nn(hot_rows(pair_a, 8), plain_terms[...])
    for c in range(8):
        remote[pl.ds(c, QUARTER, stride=8), :] = totals[:, c * LANES : (c + 1) * LANES]
    local[...] = own_totals


def reduce_kernel(
    remote, local, far, table, adjoint, far_corr, plane_in, across_in, up_in, down_in, relay_in, mate_in, cross_in,
    total, sums, send_sems, plane_sems, ring_sems, mate_sems,
):
    at = place()
    y, z, core = at["y"], at["z"], at["core"]
    barrier, count = enter(at)
    pl.semaphore_wait(barrier, count)
    send = Sender(send_sems)
    half = z // 4

    def part(cc, yy, zz, n):
        return pl.ds(pl.multiple_of(slot_of(cc, yy, zz) * 32, 32), n * 32)

    def plane(yy):
        return pl.ds(pl.multiple_of(yy * (NZ * 32), NZ * 32), NZ * 32)

    for yy in (at["across"], at["up"], at["down"], y):
        send(
            remote.at[part(1 - core, yy, 0, NZ), :],
            plane_in.at[plane(yy), :],
            plane_sems.at[yy],
            {"blk": device(y, z, 1 - core)},
        )

    def add_plane(yy):
        arrived(plane_in.at[plane(yy), :], plane_sems.at[yy], send_sems, at)
        sums[plane(yy), :] = remote[part(core, yy, 0, NZ), :] + plane_in[plane(yy), :]

    def piece(yy, zz, n):
        return pl.ds(pl.multiple_of((yy * NZ + zz) * 32, 32), n * 32)

    def halves():
        return ((0, 1 - half), (1, half))

    def ring(k, h):
        return pl.ds(pl.multiple_of(h * 128, 128), 128)

    up = {"blk": device(at["up"], z, core)}
    down = {"blk": device(at["down"], z, core)}
    add_plane(at["across"])
    for k, h in halves():
        send(sums.at[piece(at["across"], h * 4, 4), :], across_in.at[ring(k, h), :], ring_sems.at[k], up)
    add_plane(at["down"])
    for k, h in halves():
        send(sums.at[piece(at["down"], h * 4, 4), :], down_in.at[ring(k, h), :], ring_sems.at[2 + k], down)
    add_plane(at["up"])
    for k, h in halves():
        arrived(across_in.at[ring(k, h), :], ring_sems.at[k], send_sems, at)
        rows = piece(at["up"], h * 4, 4)
        sums[rows, :] = sums[rows, :] + across_in[ring(k, h), :]
        send(sums.at[rows, :], up_in.at[ring(k, h), :], ring_sems.at[4 + k], up)
    add_plane(y)

    def block(d):
        return piece(y, flip(z, d), 1)

    for k, h in halves():
        arrived(down_in.at[ring(k, h), :], ring_sems.at[2 + k], send_sems, at)
        arrived(up_in.at[ring(k, h), :], ring_sems.at[4 + k], send_sems, at)
        rows = piece(y, h * 4, 4)
        sums[rows, :] = sums[rows, :] + (down_in[ring(k, h), :] + up_in[ring(k, h), :])
        bucket, base, first = (relay_in, 0, 4) if k == 0 else (mate_in, 4, 0)
        for j in (1, 2, 3):
            send(
                sums.at[block(first + j), :],
                bucket.at[(j - 1) * 32 : j * 32, :],
                mate_sems.at[base + j - 1],
                {"blk": device(y, flip(z, j), core)},
            )
    for j in (1, 2, 3):
        arrived(relay_in.at[(j - 1) * 32 : j * 32, :], mate_sems.at[j - 1], send_sems, at)
    total[0:32, :] = (
        sums[block(4), :] + relay_in[0:32, :] + (relay_in[32:64, :] + relay_in[64:96, :])
    )
    send(total.at[0:32, :], cross_in, mate_sems.at[3], {"blk": device(y, flip(z, 4), core)})
    for j in (1, 2, 3):
        arrived(mate_in.at[(j - 1) * 32 : j * 32, :], mate_sems.at[4 + j - 1], send_sems, at)
    summed = sums[block(0), :] + mate_in[0:32, :] + (mate_in[32:64, :] + mate_in[64:96, :])
    arrived(cross_in, mate_sems.at[3], send_sems, at)
    total[32:64, :] = summed + cross_in[...]

    pieces = [total[pl.ds(32 + c, 4, stride=8), :] for c in range(8)]
    source = jnp.concatenate(pieces, axis=1) + local[0:4, :]
    even = jnp.concatenate([halve_first(source[:, :HALF]), far[:, :HALF]], axis=0)
    odd = jnp.concatenate([source[:, HALF:], far[:, HALF:]], axis=0)
    lag_even = dot3(dot_nt, split(even), table[0], table[1])
    lag_odd = dot3(dot_nt, split(odd), table[2], table[3])
    plus = (lag_even + lag_odd) * (2.0 / WIN)
    minus = (lag_even - lag_odd) * (2.0 / WIN)
    adjoint[:, :HALF] = plus[0:4, :] * (1.0 / 16.0)
    adjoint[:, HALF:] = minus[0:4, :] * (1.0 / 16.0)
    far_corr[:, :QUARTER] = minus[4:8, QUARTER:]
    far_corr[:, QUARTER:] = plus[4:8, :QUARTER]
    send.drain()


def vmem():
    return pl.BlockSpec(memory_space=pltpu.VMEM)


def smem():
    return pl.BlockSpec(memory_space=pltpu.SMEM)


def params(**kw):
    return pltpu.CompilerParams(vmem_limit_bytes=56 * 1024 * 1024, **kw)


def body(records, starts, tapers, pair_a, pair_b, pair_count, observed):
    slots = pair_a.shape[0]
    shape = jax.ShapeDtypeStruct
    table = jnp.asarray(tables())
    group, near = pl.pallas_call(
        gather_kernel,
        out_shape=(shape((2048, LANES), F32), shape((64, LANES), F32)),
        in_specs=[smem(), smem(), vmem()],
        out_specs=(vmem(), vmem()),
        scratch_shapes=[
            pltpu.VMEM((64, LANES), F32),
            pltpu.SemaphoreType.DMA((72,)),
            pltpu.SemaphoreType.DMA((64,)),
            pltpu.SemaphoreType.DMA((1,)),
        ],
        compiler_params=params(collective_id=0, has_side_effects=True),
        name="gather_windows",
    )(starts, tapers, records)
    placed = (pair_b // 4 % 2) * 128 + (pair_b // 8) * 4 + pair_b % 4
    corr, remote, local, far = pl.pallas_call(
        pairs_kernel,
        out_shape=(
            shape((slots, HALF), F32),
            shape((2048, LANES), F32),
            shape((8, WIN), F32),
            shape((4, WIN), F32),
        ),
        in_specs=[smem()] + [vmem()] * 6,
        out_specs=(vmem(),) * 4,
        scratch_shapes=[
            pltpu.VMEM((HALF, WIN), BF16),
            pltpu.VMEM((8, WIN), F32),
            pltpu.VMEM((2 * slots, WIN), BF16),
            pltpu.VMEM((2 * slots, WIN), BF16),
        ],
        compiler_params=params(),
        name="pairs",
    )(
        pair_count,
        group,
        near,
        pair_a.reshape(slots // LANES, LANES),
        placed.reshape(slots // LANES, LANES),
        observed,
        table,
    )
    adjoint, far_corr = pl.pallas_call(
        reduce_kernel,
        out_shape=(shape((4, WIN), F32), shape((4, HALF), F32)),
        in_specs=[vmem()] * 4,
        out_specs=(vmem(), vmem()),
        scratch_shapes=[
            pltpu.VMEM((1024, LANES), F32),
            pltpu.VMEM((256, LANES), F32),
            pltpu.VMEM((256, LANES), F32),
            pltpu.VMEM((256, LANES), F32),
            pltpu.VMEM((96, LANES), F32),
            pltpu.VMEM((96, LANES), F32),
            pltpu.VMEM((32, LANES), F32),
            pltpu.VMEM((64, LANES), F32),
            pltpu.VMEM((1024, LANES), F32),
            pltpu.SemaphoreType.DMA((24,)),
            pltpu.SemaphoreType.DMA((4,)),
            pltpu.SemaphoreType.DMA((6,)),
            pltpu.SemaphoreType.DMA((7,)),
        ],
        compiler_params=params(collective_id=1, has_side_effects=True),
        name="reduce_terms",
    )(remote, local, far, table)
    return corr, far_corr, adjoint


def solution(mesh):
    split_all = P(("region", "blk"))
    rows = P(("region", "blk"), None)
    return jax.shard_map(
        body,
        mesh=mesh,
        in_specs=(rows, split_all, split_all, split_all, split_all, split_all, rows),
        out_specs=(rows, rows, rows),
        check_vma=False,
    )
```

```python
import jax
import jax.numpy as jnp
import ml_dtypes
import numpy as np
from jax import lax
from jax.experimental import pallas as pl
from jax.experimental.pallas import tpu as pltpu
from jax.sharding import PartitionSpec as P

WIN = 1024
HALF = 512
QUARTER = 256
TILE = 128
LANES = 128
F32 = jnp.float32
BF16 = jnp.bfloat16
MESH = pl.DeviceIdType.MESH
NY, NZ = 4, 8


def tables():
    t = np.arange(HALF)[:, None]
    parts = []
    for parity in (0, 1):
        k = 2 * np.arange(QUARTER)[None, :] + parity
        angle = 2.0 * np.pi * ((t * k) % WIN) / WIN
        full = np.concatenate([np.cos(angle), -np.sin(angle)], axis=1)
        high = full.astype(ml_dtypes.bfloat16)
        low = (full - high.astype(np.float64)).astype(ml_dtypes.bfloat16)
        parts += [high, low]
    return np.stack(parts)


def split(x):
    high = x.astype(BF16)
    return high, (x - high.astype(F32)).astype(BF16)


def dot_nn(a, b):
    return lax.dot_general(a, b, (((1,), (0,)), ((), ())), preferred_element_type=F32)


def dot_nt(a, b):
    return lax.dot_general(a, b, (((1,), (1,)), ((), ())), preferred_element_type=F32)


def dot3(dot, pair, high, low):
    return dot(pair[0], high) + dot(pair[1], high) + dot(pair[0], low)


def place():
    blk = lax.axis_index("blk")
    core = blk % 2
    z = (blk // 2) % NZ
    y = blk // (2 * NZ)
    return {"core": core, "z": z, "y": y}


def flip(z, d):
    out = 0
    for bit in (1, 2, 4):
        own = (z // bit) % 2
        out = out + bit * ((own + (d // bit) % 2) % 2)
    return out


def device(y, z, core):
    return y * (2 * NZ) + z * 2 + core


def slot_of(core, z, y):
    return (core * NZ + z) * NY + y


def turn(y, k):
    return (y + k) % NY


def enter(at):
    y, z, core = at["y"], at["z"], at["core"]
    peers = [device(y, z, 1 - core)]
    peers += [device(turn(y, k), z, core) for k in (1, 2, 3)]
    peers += [device(y, flip(z, d), core) for d in range(1, NZ)]
    barrier = pltpu.get_barrier_semaphore()
    for peer in peers:
        pl.semaphore_signal(barrier, inc=1, device_id={"blk": peer}, device_id_type=MESH)
    return barrier, len(peers)


def window_tiles(records, starts, tapers, stage):
    lane = lax.broadcasted_iota(jnp.int32, (8, LANES), 1)
    sample = lax.broadcasted_iota(jnp.int32, (8, LANES), 0) * LANES + lane
    position = sample.astype(F32)
    tiles = []
    for i in range(4):
        base = i * 16
        for c in range(16):
            stage[base + c : base + c + 1, :] = records[i : i + 1, c * LANES : (c + 1) * LANES]
        chunks = stage[base : base + 16, :]
        start = jnp.full((16, LANES), starts[i], jnp.int32)
        for bit in (1, 2, 4, 8):
            chunks = jnp.where(start & (bit * LANES) != 0, pltpu.roll(chunks, 16 - bit, 0), chunks)
        first, second = chunks[0:8, :], pltpu.roll(chunks, 15, 0)[0:8, :]
        start = start[0:8, :]
        for bit in (1, 2, 4, 8, 16, 32, 64):
            moved_first = pltpu.roll(first, LANES - bit, 1)
            moved_second = pltpu.roll(second, LANES - bit, 1)
            taken = start & bit != 0
            first = jnp.where(taken, jnp.where(lane < LANES - bit, moved_first, moved_second), first)
            second = jnp.where(taken, moved_second, second)
        length = jnp.full((8, LANES), tapers[i], jnp.int32).astype(F32)
        shape_fn = jnp.minimum(1.0, jnp.minimum((position + 1.0) / length, (WIN - position) / length))
        tiles.append(first * shape_fn * WIN ** (-0.25))
    return tiles


class Sender:
    def __init__(self, sems):
        self.sems, self.count, self.sent = sems, 0, []

    def __call__(self, src, dst, recv, target):
        copy = pltpu.make_async_remote_copy(
            src_ref=src,
            dst_ref=dst,
            send_sem=self.sems.at[self.count],
            recv_sem=recv,
            device_id=target,
            device_id_type=MESH,
        )
        copy.start()
        self.count += 1
        self.sent.append(copy)

    def drain(self):
        for copy in self.sent:
            copy.wait_send()


def arrived(dst, recv, sems, at):
    pltpu.make_async_remote_copy(
        src_ref=dst,
        dst_ref=dst,
        send_sem=sems.at[0],
        recv_sem=recv,
        device_id={"blk": device(at["y"], at["z"], 1 - at["core"])},
        device_id_type=MESH,
    ).wait_recv()


def gather_kernel(starts, tapers, records, group, near, stage, send_sems, recv_sems, far_sem):
    at = place()
    y, z, core = at["y"], at["z"], at["core"]
    region = lax.axis_index("region")
    regions = lax.axis_size("region")
    after, before = lax.rem(region + 1, regions), lax.rem(region + regions - 1, regions)
    barrier, count = enter(at)
    for other in (after, before):
        pl.semaphore_signal(barrier, inc=1, device_id={"region": other}, device_id_type=MESH)
    tiles = window_tiles(records, starts, tapers, stage)
    mine = slot_of(core, z, y)
    for i in range(4):
        group[pl.ds(pl.multiple_of(mine * 32, 32) + i * 8, 8), :] = tiles[i]
        near[i * 8 : i * 8 + 8, :] = tiles[i]
    pl.semaphore_wait(barrier, count + 2)

    send = Sender(send_sems)

    def rows(slot):
        return group.at[pl.ds(pl.multiple_of(slot * 32, 32), 32), :]

    def pass_on(slot, yy, zz, cc):
        send(rows(slot), rows(slot), recv_sems.at[slot], {"blk": device(yy, zz, cc)})

    def take(slot):
        arrived(rows(slot), recv_sems.at[slot], send_sems, at)

    for d in (7, 6, 5, 4, 3, 2, 1):
        pass_on(mine, y, flip(z, d), core)
    for d in range(NZ):
        slot = slot_of(core, flip(z, d), y)
        if d:
            take(slot)
        for k in (2, 1, 3):
            pass_on(slot, turn(y, k), z, core)
        pass_on(slot, y, z, 1 - core)
    send(near.at[0:32, :], near.at[32:64, :], far_sem.at[0], {"region": after})
    for d in range(NZ):
        for k in (1, 3, 2):
            slot = slot_of(core, flip(z, d), turn(y, k))
            take(slot)
            pass_on(slot, y, z, 1 - core)
    for zz in range(NZ):
        for yy in range(NY):
            take(slot_of(1 - core, zz, yy))
    arrived(near.at[32:64, :], far_sem.at[0], send_sems, at)
    send.drain()


def complex_parts(x):
    return x[:, :QUARTER], x[:, QUARTER:HALF], x[:, HALF : HALF + QUARTER], x[:, HALF + QUARTER :]


def spectra_of(tile_of, table):
    pieces = [tile_of(c) for c in range(8)]
    early = jnp.concatenate(pieces[:4], axis=1)
    late = jnp.concatenate(pieces[4:], axis=1)
    even = dot3(dot_nn, split(early + late), table[0], table[1])
    odd = dot3(dot_nn, split(early - late), table[2], table[3])
    return jnp.concatenate([even, odd], axis=1)


def cross(left, right):
    lr, li, mr, mi = complex_parts(left)
    rr, ri, sr, si = complex_parts(right)
    even = jnp.concatenate([lr * rr + li * ri, li * rr - lr * ri], axis=1)
    odd = jnp.concatenate([mr * sr + mi * si, mi * sr - mr * si], axis=1)
    return even, odd


def halve_first(x):
    lane = lax.broadcasted_iota(jnp.int32, (1, HALF), 1)
    return x * jnp.where(lane == 0, 0.5, 1.0).astype(F32)


def spread(row):
    return jnp.broadcast_to(row, (LANES, LANES)).T


def pairs_kernel(
    count, group, near, pair_a, pair_b, observed, table, corr, remote, local, far, spec, own, conj_terms, plain_terms
):
    slots = corr.shape[0]
    spectra = spectra_of(lambda c: group[pl.ds(c, QUARTER, stride=8), :], table)
    high, low = split(spectra)
    spec[0:QUARTER, :] = high
    spec[QUARTER:HALF, :] = low
    ends = spectra_of(lambda c: near[pl.ds(c, 8, stride=8), :], table)
    own[...] = ends
    far_even, far_odd = cross(ends[0:4, :], ends[4:8, :])
    far[...] = jnp.concatenate([halve_first(far_even), far_odd], axis=1)
    live_count = count[0]
    lane = lax.broadcasted_iota(jnp.int32, (TILE, LANES), 1)

    def tile(i, carry):
        rows = pl.ds(pl.multiple_of(i * TILE, TILE), TILE)
        low_rows = pl.ds(pl.multiple_of(slots + i * TILE, TILE), TILE)
        b_col = spread(pair_b[pl.ds(i, 1), :])
        a_col = spread(pair_a[pl.ds(i, 1), :])
        hot = jnp.concatenate([b_col == lane, b_col == lane + LANES], axis=1).astype(F32).astype(BF16)
        target = dot_nn(hot, spec[0:QUARTER, :]) + dot_nn(hot, spec[QUARTER:HALF, :])
        pieces = []
        for c in range(8):
            cut = slice(c * LANES, (c + 1) * LANES)
            row = [jnp.broadcast_to(own[q : q + 1, cut], (TILE, LANES)) for q in range(4)]
            pieces.append(
                jnp.where(a_col == 0, row[0], jnp.where(a_col == 1, row[1], jnp.where(a_col == 2, row[2], row[3])))
            )
        source = jnp.concatenate(pieces, axis=1)
        even, odd = cross(source, target)
        lag_even = dot3(dot_nt, split(halve_first(even)), table[0], table[1])
        lag_odd = dot3(dot_nt, split(odd), table[2], table[3])
        ahead = (lag_even[:, :QUARTER] + lag_odd[:, :QUARTER]) * (2.0 / WIN)
        behind = (lag_even[:, QUARTER:] - lag_odd[:, QUARTER:]) * (2.0 / WIN)
        number = lax.broadcasted_iota(jnp.int32, (TILE, QUARTER), 0) + i * TILE
        live = number < live_count
        corr[rows, 0:QUARTER] = jnp.where(live, behind, 0.0)
        corr[rows, QUARTER:HALF] = jnp.where(live, ahead, 0.0)
        res_behind = split(jnp.where(live, behind - observed[rows, 0:QUARTER], 0.0))
        res_ahead = split(jnp.where(live, ahead - observed[rows, QUARTER:HALF], 0.0))
        plus = [jnp.concatenate([res_ahead[q], res_behind[q]], axis=1) for q in (0, 1)]
        minus = [jnp.concatenate([res_ahead[q], -res_behind[q]], axis=1) for q in (0, 1)]
        mis_even = dot3(dot_nn, plus, table[0], table[1])
        mis_odd = dot3(dot_nn, minus, table[2], table[3])
        for p, mis in ((0, mis_even), (1, mis_odd)):
            mr, mi = mis[:, :QUARTER], mis[:, QUARTER:]
            base = p * HALF
            sr, si = source[:, base : base + QUARTER], source[:, base + QUARTER : base + HALF]
            tr, ti = target[:, base : base + QUARTER], target[:, base + QUARTER : base + HALF]
            for terms, re, im in (
                (conj_terms, mr * sr + mi * si, mr * si - mi * sr),
                (plain_terms, mr * tr - mi * ti, mr * ti + mi * tr),
            ):
                for offset, part in ((0, re), (QUARTER, im)):
                    part_high, part_low = split(part)
                    cut = slice(base + offset, base + offset + QUARTER)
                    terms[rows, cut] = part_high
                    terms[low_rows, cut] = part_low
        return carry

    lax.fori_loop(0, slots // TILE, tile, 0)

    def hot_rows(index, height):
        down = lax.broadcasted_iota(jnp.int32, (height, LANES), 0)
        cols = [
            (jnp.broadcast_to(index[i : i + 1, :], (height, LANES)) == down).astype(F32).astype(BF16)
            for i in range(slots // LANES)
        ]
        return jnp.concatenate(cols + cols, axis=1)

    totals = dot_nn(hot_rows(pair_b, QUARTER), conj_terms[...])
    own_totals = dot_nn(hot_rows(pair_a, 8), plain_terms[...])
    for c in range(8):
        remote[pl.ds(c, QUARTER, stride=8), :] = totals[:, c * LANES : (c + 1) * LANES]
    local[...] = own_totals


def reduce_kernel(
    remote, local, far, table, adjoint, far_corr, plane_in, ring_in, mate_in, sums, total,
    send_sems, plane_sems, ring_sems, mate_sems,
):
    at = place()
    y, z, core = at["y"], at["z"], at["core"]
    barrier, count = enter(at)
    pl.semaphore_wait(barrier, count)
    send = Sender(send_sems)
    outward = (7, 6, 5, 4, 3, 2, 1, 0)

    def part(cc, zz):
        return pl.ds(pl.multiple_of(slot_of(cc, zz, 0) * 32, 32), NY * 32)

    def block(zz, yy):
        return pl.ds(pl.multiple_of(slot_of(0, zz, yy) * 32, 32), 32)

    def ring(k, d):
        return slice(((k - 1) * NZ + d) * 32, ((k - 1) * NZ + d + 1) * 32)

    def mate(d):
        return slice(d * 32, d * 32 + 32)

    for d in outward:
        zz = flip(z, d)
        send(
            remote.at[part(1 - core, zz), :],
            plane_in.at[part(0, zz), :],
            plane_sems.at[d],
            {"blk": device(y, z, 1 - core)},
        )
    for d in outward:
        zz = flip(z, d)
        arrived(plane_in.at[part(0, zz), :], plane_sems.at[d], send_sems, at)
        sums[part(0, zz), :] = remote[part(core, zz), :] + plane_in[part(0, zz), :]
        for k in (2, 1, 3):
            send(
                sums.at[block(zz, turn(y, k)), :],
                ring_in.at[ring(k, d), :],
                ring_sems.at[(k - 1) * NZ + d],
                {"blk": device(turn(y, k), z, core)},
            )
    for d in outward:
        for k in (1, 3, 2):
            arrived(ring_in.at[ring(k, d), :], ring_sems.at[(k - 1) * NZ + d], send_sems, at)
        total[mate(d), :] = (
            sums[block(flip(z, d), y), :] + ring_in[ring(1, d), :] + (ring_in[ring(2, d), :] + ring_in[ring(3, d), :])
        )
        if d:
            send(
                total.at[mate(d), :], mate_in.at[mate(d), :], mate_sems.at[d], {"blk": device(y, flip(z, d), core)}
            )
    summed = total[mate(0), :]
    for d in (1, 2, 3, 4, 5, 6, 7):
        arrived(mate_in.at[mate(d), :], mate_sems.at[d], send_sems, at)
        summed = summed + mate_in[mate(d), :]
    total[mate(0), :] = summed

    pieces = [total[pl.ds(c, 4, stride=8), :] for c in range(8)]
    source = jnp.concatenate(pieces, axis=1) + local[0:4, :]
    even = jnp.concatenate([halve_first(source[:, :HALF]), far[:, :HALF]], axis=0)
    odd = jnp.concatenate([source[:, HALF:], far[:, HALF:]], axis=0)
    lag_even = dot3(dot_nt, split(even), table[0], table[1])
    lag_odd = dot3(dot_nt, split(odd), table[2], table[3])
    plus = (lag_even + lag_odd) * (2.0 / WIN)
    minus = (lag_even - lag_odd) * (2.0 / WIN)
    adjoint[:, :HALF] = plus[0:4, :] * (1.0 / 16.0)
    adjoint[:, HALF:] = minus[0:4, :] * (1.0 / 16.0)
    far_corr[:, :QUARTER] = minus[4:8, QUARTER:]
    far_corr[:, QUARTER:] = plus[4:8, :QUARTER]
    send.drain()


def vmem():
    return pl.BlockSpec(memory_space=pltpu.VMEM)


def smem():
    return pl.BlockSpec(memory_space=pltpu.SMEM)


def params(**kw):
    return pltpu.CompilerParams(vmem_limit_bytes=56 * 1024 * 1024, **kw)


def body(records, starts, tapers, pair_a, pair_b, pair_count, observed):
    slots = pair_a.shape[0]
    shape = jax.ShapeDtypeStruct
    table = jnp.asarray(tables())
    group, near = pl.pallas_call(
        gather_kernel,
        out_shape=(shape((2048, LANES), F32), shape((64, LANES), F32)),
        in_specs=[smem(), smem(), vmem()],
        out_specs=(vmem(), vmem()),
        scratch_shapes=[
            pltpu.VMEM((64, LANES), F32),
            pltpu.SemaphoreType.DMA((72,)),
            pltpu.SemaphoreType.DMA((64,)),
            pltpu.SemaphoreType.DMA((1,)),
        ],
        compiler_params=params(collective_id=0, has_side_effects=True),
        name="gather_windows",
    )(starts, tapers, records)
    placed = (pair_b // 4 % 2) * 128 + (pair_b // 8 % NZ) * 16 + (pair_b // 64) * 4 + pair_b % 4
    corr, remote, local, far = pl.pallas_call(
        pairs_kernel,
        out_shape=(
            shape((slots, HALF), F32),
            shape((2048, LANES), F32),
            shape((8, WIN), F32),
            shape((4, WIN), F32),
        ),
        in_specs=[smem()] + [vmem()] * 6,
        out_specs=(vmem(),) * 4,
        scratch_shapes=[
            pltpu.VMEM((HALF, WIN), BF16),
            pltpu.VMEM((8, WIN), F32),
            pltpu.VMEM((2 * slots, WIN), BF16),
            pltpu.VMEM((2 * slots, WIN), BF16),
        ],
        compiler_params=params(),
        name="pairs",
    )(
        pair_count,
        group,
        near,
        pair_a.reshape(slots // LANES, LANES),
        placed.reshape(slots // LANES, LANES),
        observed,
        table,
    )
    adjoint, far_corr = pl.pallas_call(
        reduce_kernel,
        out_shape=(shape((4, WIN), F32), shape((4, HALF), F32)),
        in_specs=[vmem()] * 4,
        out_specs=(vmem(), vmem()),
        scratch_shapes=[
            pltpu.VMEM((1024, LANES), F32),
            pltpu.VMEM((768, LANES), F32),
            pltpu.VMEM((256, LANES), F32),
            pltpu.VMEM((1024, LANES), F32),
            pltpu.VMEM((256, LANES), F32),
            pltpu.SemaphoreType.DMA((40,)),
            pltpu.SemaphoreType.DMA((8,)),
            pltpu.SemaphoreType.DMA((24,)),
            pltpu.SemaphoreType.DMA((8,)),
        ],
        compiler_params=params(collective_id=1, has_side_effects=True),
        name="reduce_terms",
    )(remote, local, far, table)
    return corr, far_corr, adjoint


def solution(mesh):
    split_all = P(("region", "blk"))
    rows = P(("region", "blk"), None)
    return jax.shard_map(
        body,
        mesh=mesh,
        in_specs=(rows, split_all, split_all, split_all, split_all, split_all, rows),
        out_specs=(rows, rows, rows),
        check_vma=False,
    )
```

```python
import jax
import jax.numpy as jnp
import ml_dtypes
import numpy as np
from jax import lax
from jax.experimental import pallas as pl
from jax.experimental.pallas import tpu as pltpu
from jax.sharding import PartitionSpec as P

WIN = 1024
HALF = 512
QUARTER = 256
TILE = 768
LANES = 128
F32 = jnp.float32
BF16 = jnp.bfloat16
MESH = pl.DeviceIdType.MESH
NY, NZ = 4, 8


def tables():
    def table(t, k):
        angle = 2.0 * np.pi * ((t[:, None] * k[None, :]) % WIN) / WIN
        full = np.concatenate([np.cos(angle), -np.sin(angle)], axis=1)
        high = full.astype(ml_dtypes.bfloat16)
        return [high, (full - high.astype(np.float64)).astype(ml_dtypes.bfloat16)]

    four = 4 * np.arange(LANES)
    quarter = np.stack(table(np.arange(QUARTER), four) + table(np.arange(QUARTER), four + 2))
    return quarter, np.stack(table(np.arange(HALF), 2 * np.arange(QUARTER) + 1))


def split(x):
    high = x.astype(BF16)
    return high, (x - high.astype(F32)).astype(BF16)


def dot_nn(a, b):
    return lax.dot_general(a, b, (((1,), (0,)), ((), ())), preferred_element_type=F32)


def dot_nt(a, b):
    return lax.dot_general(a, b, (((1,), (1,)), ((), ())), preferred_element_type=F32)


def dot3(dot, pair, high, low):
    return dot(pair[0], high) + dot(pair[1], high) + dot(pair[0], low)


def place():
    blk = lax.axis_index("blk")
    core = blk % 2
    z = (blk // 2) % NZ
    y = blk // (2 * NZ)
    return {"core": core, "z": z, "y": y}


def flip(z, d):
    out = 0
    for bit in (1, 2, 4):
        own = (z // bit) % 2
        out = out + bit * ((own + (d // bit) % 2) % 2)
    return out


def device(y, z, core):
    return y * (2 * NZ) + z * 2 + core


def slot_of(core, z, y):
    return (core * NZ + z) * NY + y


def turn(y, k):
    return (y + k) % NY


def enter(at):
    y, z, core = at["y"], at["z"], at["core"]
    peers = [device(y, z, 1 - core)]
    peers += [device(turn(y, k), z, core) for k in (1, 2, 3)]
    peers += [device(y, flip(z, d), core) for d in range(1, NZ)]
    barrier = pltpu.get_barrier_semaphore()
    for peer in peers:
        pl.semaphore_signal(barrier, inc=1, device_id={"blk": peer}, device_id_type=MESH)
    return barrier, len(peers)


def window_tiles(records, starts, tapers, stage):
    lane = lax.broadcasted_iota(jnp.int32, (8, LANES), 1)
    sample = lax.broadcasted_iota(jnp.int32, (8, LANES), 0) * LANES + lane
    position = sample.astype(F32)
    tiles = []
    for i in range(4):
        base = i * 16
        for c in range(16):
            stage[base + c : base + c + 1, :] = records[i : i + 1, c * LANES : (c + 1) * LANES]
        chunks = stage[base : base + 16, :]
        start = jnp.full((16, LANES), starts[i], jnp.int32)
        for bit in (1, 2, 4, 8):
            chunks = jnp.where(start & (bit * LANES) != 0, pltpu.roll(chunks, 16 - bit, 0), chunks)
        first, second = chunks[0:8, :], pltpu.roll(chunks, 15, 0)[0:8, :]
        start = start[0:8, :]
        for bit in (1, 2, 4, 8, 16, 32, 64):
            moved_first = pltpu.roll(first, LANES - bit, 1)
            moved_second = pltpu.roll(second, LANES - bit, 1)
            taken = start & bit != 0
            first = jnp.where(taken, jnp.where(lane < LANES - bit, moved_first, moved_second), first)
            second = jnp.where(taken, moved_second, second)
        length = jnp.full((8, LANES), tapers[i], jnp.int32).astype(F32)
        shape_fn = jnp.minimum(1.0, jnp.minimum((position + 1.0) / length, (WIN - position) / length))
        tiles.append(first * shape_fn * WIN ** (-0.25))
    return tiles


class Sender:
    def __init__(self, sems):
        self.sems, self.count, self.sent = sems, 0, []

    def __call__(self, src, dst, recv, target):
        copy = pltpu.make_async_remote_copy(
            src_ref=src,
            dst_ref=dst,
            send_sem=self.sems.at[self.count],
            recv_sem=recv,
            device_id=target,
            device_id_type=MESH,
        )
        copy.start()
        self.count += 1
        self.sent.append(copy)

    def drain(self):
        for copy in self.sent:
            copy.wait_send()


def arrived(dst, recv, sems, at):
    pltpu.make_async_remote_copy(
        src_ref=dst,
        dst_ref=dst,
        send_sem=sems.at[0],
        recv_sem=recv,
        device_id={"blk": device(at["y"], at["z"], 1 - at["core"])},
        device_id_type=MESH,
    ).wait_recv()


def gather_kernel(starts, tapers, records, group, near, stage, send_sems, recv_sems):
    at = place()
    y, z, core = at["y"], at["z"], at["core"]
    barrier, count = enter(at)
    tiles = window_tiles(records, starts, tapers, stage)
    mine = slot_of(core, z, y)
    for i in range(4):
        group[pl.ds(pl.multiple_of(mine * 32, 32) + i * 8, 8), :] = tiles[i]
        near[i * 8 : i * 8 + 8, :] = tiles[i]
    pl.semaphore_wait(barrier, count)

    send = Sender(send_sems)

    def rows(slot):
        return group.at[pl.ds(pl.multiple_of(slot * 32, 32), 32), :]

    def pass_on(slot, yy, zz, cc):
        send(rows(slot), rows(slot), recv_sems.at[slot], {"blk": device(yy, zz, cc)})

    def take(slot):
        arrived(rows(slot), recv_sems.at[slot], send_sems, at)

    for d in (7, 6, 5, 4, 3, 2, 1):
        pass_on(mine, y, flip(z, d), core)
    for d in range(NZ):
        slot = slot_of(core, flip(z, d), y)
        if d:
            take(slot)
        for k in (2, 1, 3):
            pass_on(slot, turn(y, k), z, core)
        pass_on(slot, y, z, 1 - core)
    for d in range(NZ):
        for k in (1, 3, 2):
            slot = slot_of(core, flip(z, d), turn(y, k))
            take(slot)
            pass_on(slot, y, z, 1 - core)
    for zz in range(NZ):
        for yy in range(NY):
            take(slot_of(1 - core, zz, yy))
    send.drain()


SEGMENTS = ((0, LANES), (QUARTER, LANES), (HALF, QUARTER))


def spectra_of(tile_of, quarter, odd):
    pieces = [tile_of(c) for c in range(8)]
    early = jnp.concatenate(pieces[:4], axis=1)
    late = jnp.concatenate(pieces[4:], axis=1)
    both = early + late
    front, back = both[:, :QUARTER], both[:, QUARTER:]
    return jnp.concatenate(
        [
            dot3(dot_nn, split(front + back), quarter[0], quarter[1]),
            dot3(dot_nn, split(front - back), quarter[2], quarter[3]),
            dot3(dot_nn, split(early - late), odd[0], odd[1]),
        ],
        axis=1,
    )


def cross(left, right):
    out = []
    for base, n in SEGMENTS:
        lr, li = left[:, base : base + n], left[:, base + n : base + 2 * n]
        rr, ri = right[:, base : base + n], right[:, base + n : base + 2 * n]
        out.append(jnp.concatenate([lr * rr + li * ri, li * rr - lr * ri], axis=1))
    return out


def halve_first(x):
    lane = lax.broadcasted_iota(jnp.int32, (1, x.shape[1]), 1)
    return x * jnp.where(lane == 0, 0.5, 1.0).astype(F32)


def unpack(zero, two, rest, quarter, odd):
    p0 = dot3(dot_nt, split(halve_first(zero)), quarter[0], quarter[1])
    p2 = dot3(dot_nt, split(two), quarter[2], quarter[3])
    return p0 + p2, p0 - p2, dot3(dot_nt, split(rest), odd[0], odd[1])


def spread(row):
    return jnp.broadcast_to(row, (LANES, LANES)).T


def columns(index, first):
    rows = [spread(index[first + j : first + j + 1, :]) for j in range(TILE // LANES)]
    return jnp.concatenate(rows, axis=0)


def pairs_kernel(
    count, group, pair_a, pair_b, observed, quarter, odd, corr, remote, local,
    spec, full, conj_terms, plain_terms, target_lags, lags, in_sem, out_sem,
):
    slots = corr.shape[0]
    at = place()
    fetch = pltpu.make_async_copy(observed, target_lags, in_sem)
    fetch.start()
    spectra = spectra_of(lambda c: group[pl.ds(c, QUARTER, stride=8), :], quarter, odd)
    full[...] = spectra
    high, low = split(spectra)
    spec[0:QUARTER, :] = high
    spec[QUARTER:HALF, :] = low
    mine = slot_of(at["core"], at["z"], at["y"]) * 4
    b = pair_b[...]
    placed = ((b >> 2) & 1) * 128 + ((b >> 3) & 7) * 16 + (b >> 6) * 4 + (b & 3)
    live_count = count[0]
    lane = lax.broadcasted_iota(jnp.int32, (TILE, LANES), 1)
    own = [full[pl.ds(mine + q, 1), :] for q in range(4)]
    stores = []

    for i in range(slots // TILE):
        rows = slice(i * TILE, (i + 1) * TILE)
        low_rows = slice(slots + i * TILE, slots + (i + 1) * TILE)
        b_col = columns(placed, i * (TILE // LANES))
        a_col = columns(pair_a, i * (TILE // LANES))
        hot = jnp.concatenate([b_col == lane, b_col == lane + LANES], axis=1).astype(F32).astype(BF16)
        target = dot_nn(hot, spec[0:QUARTER, :]) + dot_nn(hot, spec[QUARTER:HALF, :])
        pieces = []
        for c in range(8):
            row = [jnp.broadcast_to(own[q][:, c * LANES : (c + 1) * LANES], (TILE, LANES)) for q in range(4)]
            pieces.append(
                jnp.where(a_col == 0, row[0], jnp.where(a_col == 1, row[1], jnp.where(a_col == 2, row[2], row[3])))
            )
        source = jnp.concatenate(pieces, axis=1)
        front, back, rest = unpack(*cross(source, target), quarter, odd)
        ahead = (front + rest[:, :QUARTER]) * (2.0 / WIN)
        behind = (back - rest[:, QUARTER:]) * (2.0 / WIN)
        live = lax.broadcasted_iota(jnp.int32, (TILE, QUARTER), 0) + i * TILE < live_count
        lags[rows, 0:QUARTER] = jnp.where(live, behind, 0.0)
        lags[rows, QUARTER:HALF] = jnp.where(live, ahead, 0.0)
        if i == 0:
            fetch.wait()
        res_behind = jnp.where(live, behind - target_lags[rows, 0:QUARTER], 0.0)
        res_ahead = jnp.where(live, ahead - target_lags[rows, QUARTER:HALF], 0.0)
        store = pltpu.make_async_copy(lags.at[rows, :], corr.at[rows, :], out_sem.at[i])
        store.start()
        stores.append(store)
        misfit = (
            dot3(dot_nn, split(res_ahead + res_behind), quarter[0], quarter[1]),
            dot3(dot_nn, split(res_ahead - res_behind), quarter[2], quarter[3]),
            dot3(dot_nn, split(jnp.concatenate([res_ahead, -res_behind], axis=1)), odd[0], odd[1]),
        )
        for (base, n), mis in zip(SEGMENTS, misfit):
            mr, mi = mis[:, :n], mis[:, n:]
            sr, si = source[:, base : base + n], source[:, base + n : base + 2 * n]
            tr, ti = target[:, base : base + n], target[:, base + n : base + 2 * n]
            for terms, re, im in (
                (conj_terms, mr * sr + mi * si, mr * si - mi * sr),
                (plain_terms, mr * tr - mi * ti, mr * ti + mi * tr),
            ):
                for offset, part in ((0, re), (n, im)):
                    part_high, part_low = split(part)
                    cut = slice(base + offset, base + offset + n)
                    terms[rows, cut] = part_high
                    terms[low_rows, cut] = part_low

    def hot_rows(index, height):
        down = lax.broadcasted_iota(jnp.int32, (height, LANES), 0)
        cols = [
            (jnp.broadcast_to(index[i : i + 1, :], (height, LANES)) == down).astype(F32).astype(BF16)
            for i in range(slots // LANES)
        ]
        return jnp.concatenate(cols + cols, axis=1)

    totals = dot_nn(hot_rows(placed, QUARTER), conj_terms[...])
    own_totals = dot_nn(hot_rows(pair_a, 8), plain_terms[...])
    for c in range(8):
        remote[pl.ds(c, QUARTER, stride=8), :] = totals[:, c * LANES : (c + 1) * LANES]
    local[...] = own_totals
    for store in stores:
        store.wait()


def reduce_kernel(
    remote, local, near, quarter_hbm, odd_hbm, adjoint, far_corr, plane_in, ring_in, mate_in, sums, total, ends,
    quarter, odd, send_sems, plane_sems, ring_sems, mate_sems, far_sem, table_sems,
):
    at = place()
    y, z, core = at["y"], at["z"], at["core"]
    region = lax.axis_index("region")
    regions = lax.axis_size("region")
    after, before = lax.rem(region + 1, regions), lax.rem(region + regions - 1, regions)
    barrier, count = enter(at)
    for other in (after, before):
        pl.semaphore_signal(barrier, inc=1, device_id={"region": other}, device_id_type=MESH)
    fetches = [
        pltpu.make_async_copy(quarter_hbm, quarter, table_sems.at[0]),
        pltpu.make_async_copy(odd_hbm, odd, table_sems.at[1]),
    ]
    for fetch in fetches:
        fetch.start()
    ends[0:32, :] = near[...]
    pl.semaphore_wait(barrier, count + 2)
    send = Sender(send_sems)
    outward = (7, 6, 5, 4, 3, 2, 1, 0)

    def part(cc, zz):
        return pl.ds(pl.multiple_of(slot_of(cc, zz, 0) * 32, 32), NY * 32)

    def block(zz, yy):
        return pl.ds(pl.multiple_of(slot_of(0, zz, yy) * 32, 32), 32)

    def ring(k, d):
        return slice(((k - 1) * NZ + d) * 32, ((k - 1) * NZ + d + 1) * 32)

    def mate(d):
        return slice(d * 32, d * 32 + 32)

    for d in outward:
        zz = flip(z, d)
        send(
            remote.at[part(1 - core, zz), :],
            plane_in.at[part(0, zz), :],
            plane_sems.at[d],
            {"blk": device(y, z, 1 - core)},
        )
    send(near, ends.at[32:64, :], far_sem.at[0], {"region": after})
    for d in outward:
        zz = flip(z, d)
        arrived(plane_in.at[part(0, zz), :], plane_sems.at[d], send_sems, at)
        sums[part(0, zz), :] = remote[part(core, zz), :] + plane_in[part(0, zz), :]
        for k in (2, 1, 3):
            send(
                sums.at[block(zz, turn(y, k)), :],
                ring_in.at[ring(k, d), :],
                ring_sems.at[(k - 1) * NZ + d],
                {"blk": device(turn(y, k), z, core)},
            )
    for d in outward:
        for k in (1, 3, 2):
            arrived(ring_in.at[ring(k, d), :], ring_sems.at[(k - 1) * NZ + d], send_sems, at)
        total[mate(d), :] = (
            sums[block(flip(z, d), y), :] + ring_in[ring(1, d), :] + (ring_in[ring(2, d), :] + ring_in[ring(3, d), :])
        )
        if d:
            send(
                total.at[mate(d), :], mate_in.at[mate(d), :], mate_sems.at[d], {"blk": device(y, flip(z, d), core)}
            )
    for fetch in fetches:
        fetch.wait()
    arrived(ends.at[32:64, :], far_sem.at[0], send_sems, at)
    spectra = spectra_of(lambda c: ends[pl.ds(c, 8, stride=8), :], quarter, odd)
    far = cross(spectra[0:4, :], spectra[4:8, :])
    summed = total[mate(0), :]
    for d in (1, 2, 3, 4, 5, 6, 7):
        arrived(mate_in.at[mate(d), :], mate_sems.at[d], send_sems, at)
        summed = summed + mate_in[mate(d), :]
    total[mate(0), :] = summed

    pieces = [total[pl.ds(c, 4, stride=8), :] for c in range(8)]
    source = jnp.concatenate(pieces, axis=1) + local[0:4, :]
    front, back, rest = unpack(
        *[
            jnp.concatenate([source[:, base : base + 2 * n], far[i]], axis=0)
            for i, (base, n) in enumerate(SEGMENTS)
        ],
        quarter,
        odd,
    )
    plus = (jnp.concatenate([front, back], axis=1) + rest) * (2.0 / WIN)
    minus = (jnp.concatenate([front, back], axis=1) - rest) * (2.0 / WIN)
    adjoint[:, :HALF] = plus[0:4, :] * (1.0 / 16.0)
    adjoint[:, HALF:] = minus[0:4, :] * (1.0 / 16.0)
    far_corr[:, :QUARTER] = minus[4:8, QUARTER:]
    far_corr[:, QUARTER:] = plus[4:8, :QUARTER]
    send.drain()


def vmem():
    return pl.BlockSpec(memory_space=pltpu.VMEM)


def smem():
    return pl.BlockSpec(memory_space=pltpu.SMEM)


def anywhere():
    return pl.BlockSpec(memory_space=pl.ANY)


def params(**kw):
    return pltpu.CompilerParams(vmem_limit_bytes=56 * 1024 * 1024, **kw)


def body(records, starts, tapers, pair_a, pair_b, pair_count, observed):
    slots = pair_a.shape[0]
    shape = jax.ShapeDtypeStruct
    quarter, odd = (jnp.asarray(table) for table in tables())
    group, near = pl.pallas_call(
        gather_kernel,
        out_shape=(shape((2048, LANES), F32), shape((32, LANES), F32)),
        in_specs=[smem(), smem(), vmem()],
        out_specs=(vmem(), vmem()),
        scratch_shapes=[
            pltpu.VMEM((64, LANES), F32),
            pltpu.SemaphoreType.DMA((72,)),
            pltpu.SemaphoreType.DMA((64,)),
        ],
        compiler_params=params(collective_id=0, has_side_effects=True),
        name="gather_windows",
    )(starts, tapers, records)
    corr, remote, local = pl.pallas_call(
        pairs_kernel,
        out_shape=(
            shape((slots, HALF), F32),
            shape((2048, LANES), F32),
            shape((8, WIN), F32),
        ),
        in_specs=[smem()] + [vmem()] * 3 + [anywhere()] + [vmem()] * 2,
        out_specs=(anywhere(), vmem(), vmem()),
        scratch_shapes=[
            pltpu.VMEM((HALF, WIN), BF16),
            pltpu.VMEM((QUARTER, WIN), F32),
            pltpu.VMEM((2 * slots, WIN), BF16),
            pltpu.VMEM((2 * slots, WIN), BF16),
            pltpu.VMEM((slots, HALF), F32),
            pltpu.VMEM((slots, HALF), F32),
            pltpu.SemaphoreType.DMA,
            pltpu.SemaphoreType.DMA((slots // TILE,)),
        ],
        compiler_params=params(),
        name="pairs",
    )(
        pair_count,
        group,
        pair_a.reshape(slots // LANES, LANES),
        pair_b.reshape(slots // LANES, LANES),
        observed,
        quarter,
        odd,
    )
    adjoint, far_corr = pl.pallas_call(
        reduce_kernel,
        out_shape=(shape((4, WIN), F32), shape((4, HALF), F32)),
        in_specs=[vmem()] * 3 + [anywhere()] * 2,
        out_specs=(vmem(), vmem()),
        scratch_shapes=[
            pltpu.VMEM((1024, LANES), F32),
            pltpu.VMEM((768, LANES), F32),
            pltpu.VMEM((256, LANES), F32),
            pltpu.VMEM((1024, LANES), F32),
            pltpu.VMEM((256, LANES), F32),
            pltpu.VMEM((64, LANES), F32),
            pltpu.VMEM(quarter.shape, BF16),
            pltpu.VMEM(odd.shape, BF16),
            pltpu.SemaphoreType.DMA((40,)),
            pltpu.SemaphoreType.DMA((8,)),
            pltpu.SemaphoreType.DMA((24,)),
            pltpu.SemaphoreType.DMA((8,)),
            pltpu.SemaphoreType.DMA((1,)),
            pltpu.SemaphoreType.DMA((2,)),
        ],
        compiler_params=params(collective_id=1, has_side_effects=True),
        name="reduce_terms",
    )(remote, local, near, quarter, odd)
    return corr, far_corr, adjoint


def solution(mesh):
    split_all = P(("region", "blk"))
    rows = P(("region", "blk"), None)
    return jax.shard_map(
        body,
        mesh=mesh,
        in_specs=(rows, split_all, split_all, split_all, split_all, split_all, rows),
        out_specs=(rows, rows, rows),
        check_vma=False,
    )
```

```python
import jax
import jax.numpy as jnp
import ml_dtypes
import numpy as np
from jax import lax
from jax.experimental import pallas as pl
from jax.experimental.pallas import tpu as pltpu
from jax.sharding import PartitionSpec as P

WIN = 1024
HALF = 512
QUARTER = 256
TILE = 768
LANES = 128
F32 = jnp.float32
BF16 = jnp.bfloat16
MESH = pl.DeviceIdType.MESH
NY, NZ = 4, 8


def tables():
    def table(t, k):
        angle = 2.0 * np.pi * ((t[:, None] * k[None, :]) % WIN) / WIN
        full = np.concatenate([np.cos(angle), -np.sin(angle)], axis=1)
        high = full.astype(ml_dtypes.bfloat16)
        return [high, (full - high.astype(np.float64)).astype(ml_dtypes.bfloat16)]

    four = 4 * np.arange(LANES)
    quarter = np.stack(table(np.arange(QUARTER), four) + table(np.arange(QUARTER), four + 2))
    return quarter, np.stack(table(np.arange(HALF), 2 * np.arange(QUARTER) + 1))


def split(x):
    high = x.astype(BF16)
    return high, (x - high.astype(F32)).astype(BF16)


def dot_nn(a, b):
    return lax.dot_general(a, b, (((1,), (0,)), ((), ())), preferred_element_type=F32)


def dot_nt(a, b):
    return lax.dot_general(a, b, (((1,), (1,)), ((), ())), preferred_element_type=F32)


def dot3(dot, pair, high, low):
    return dot(pair[0], high) + dot(pair[1], high) + dot(pair[0], low)


def place():
    blk = lax.axis_index("blk")
    core = blk % 2
    z = (blk // 2) % NZ
    y = blk // (2 * NZ)
    return {"core": core, "z": z, "y": y}


def flip(z, d):
    out = 0
    for bit in (1, 2, 4):
        own = (z // bit) % 2
        out = out + bit * ((own + (d // bit) % 2) % 2)
    return out


def device(y, z, core):
    return y * (2 * NZ) + z * 2 + core


def slot_of(core, z, y):
    return (core * NZ + z) * NY + y


def turn(y, k):
    return (y + k) % NY


def enter(at):
    y, z, core = at["y"], at["z"], at["core"]
    peers = [device(y, z, 1 - core)]
    peers += [device(turn(y, k), z, core) for k in (1, 2, 3)]
    peers += [device(y, flip(z, d), core) for d in range(1, NZ)]
    barrier = pltpu.get_barrier_semaphore()
    for peer in peers:
        pl.semaphore_signal(barrier, inc=1, device_id={"blk": peer}, device_id_type=MESH)
    return barrier, len(peers)


def window_tiles(records, starts, tapers, stage):
    lane = lax.broadcasted_iota(jnp.int32, (8, LANES), 1)
    sample = lax.broadcasted_iota(jnp.int32, (8, LANES), 0) * LANES + lane
    position = sample.astype(F32)
    tiles = []
    for i in range(4):
        base = i * 16
        for c in range(16):
            stage[base + c : base + c + 1, :] = records[i : i + 1, c * LANES : (c + 1) * LANES]
        chunks = stage[base : base + 16, :]
        start = jnp.full((16, LANES), starts[i], jnp.int32)
        for bit in (1, 2, 4, 8):
            chunks = jnp.where(start & (bit * LANES) != 0, pltpu.roll(chunks, 16 - bit, 0), chunks)
        first, second = chunks[0:8, :], pltpu.roll(chunks, 15, 0)[0:8, :]
        start = start[0:8, :]
        for bit in (1, 2, 4, 8, 16, 32, 64):
            moved_first = pltpu.roll(first, LANES - bit, 1)
            moved_second = pltpu.roll(second, LANES - bit, 1)
            taken = start & bit != 0
            first = jnp.where(taken, jnp.where(lane < LANES - bit, moved_first, moved_second), first)
            second = jnp.where(taken, moved_second, second)
        length = jnp.full((8, LANES), tapers[i], jnp.int32).astype(F32)
        shape_fn = jnp.minimum(1.0, jnp.minimum((position + 1.0) / length, (WIN - position) / length))
        tiles.append(first * shape_fn * WIN ** (-0.25))
    return tiles


class Sender:
    def __init__(self, sems):
        self.sems, self.count, self.sent = sems, 0, []

    def __call__(self, src, dst, recv, target):
        copy = pltpu.make_async_remote_copy(
            src_ref=src,
            dst_ref=dst,
            send_sem=self.sems.at[self.count],
            recv_sem=recv,
            device_id=target,
            device_id_type=MESH,
        )
        copy.start()
        self.count += 1
        self.sent.append(copy)

    def drain(self):
        for copy in self.sent:
            copy.wait_send()


def arrived(dst, recv, sems, at):
    pltpu.make_async_remote_copy(
        src_ref=dst,
        dst_ref=dst,
        send_sem=sems.at[0],
        recv_sem=recv,
        device_id={"blk": device(at["y"], at["z"], 1 - at["core"])},
        device_id_type=MESH,
    ).wait_recv()


def gather_kernel(starts, tapers, records, group, near, stage, send_sems, recv_sems):
    at = place()
    y, z, core = at["y"], at["z"], at["core"]
    barrier, count = enter(at)
    tiles = window_tiles(records, starts, tapers, stage)
    mine = slot_of(core, z, y)
    for i in range(4):
        group[pl.ds(pl.multiple_of(mine * 32, 32) + i * 8, 8), :] = tiles[i]
        near[i * 8 : i * 8 + 8, :] = tiles[i]
    pl.semaphore_wait(barrier, count)

    send = Sender(send_sems)

    def rows(slot):
        return group.at[pl.ds(pl.multiple_of(slot * 32, 32), 32), :]

    def pass_on(slot, yy, zz, cc):
        send(rows(slot), rows(slot), recv_sems.at[slot], {"blk": device(yy, zz, cc)})

    def take(slot):
        arrived(rows(slot), recv_sems.at[slot], send_sems, at)

    for d in (7, 6, 5, 4, 3, 2, 1):
        pass_on(mine, y, flip(z, d), core)
    for d in range(NZ):
        slot = slot_of(core, flip(z, d), y)
        if d:
            take(slot)
        for k in (2, 1, 3):
            pass_on(slot, turn(y, k), z, core)
        pass_on(slot, y, z, 1 - core)
    for d in range(NZ):
        for k in (1, 3, 2):
            slot = slot_of(core, flip(z, d), turn(y, k))
            take(slot)
            pass_on(slot, y, z, 1 - core)
    for zz in range(NZ):
        for yy in range(NY):
            take(slot_of(1 - core, zz, yy))
    send.drain()


SEGMENTS = ((0, LANES), (QUARTER, LANES), (HALF, QUARTER))


def spectra_of(tile_of, quarter, odd):
    pieces = [tile_of(c) for c in range(8)]
    early = jnp.concatenate(pieces[:4], axis=1)
    late = jnp.concatenate(pieces[4:], axis=1)
    both = early + late
    front, back = both[:, :QUARTER], both[:, QUARTER:]
    return jnp.concatenate(
        [
            dot3(dot_nn, split(front + back), quarter[0], quarter[1]),
            dot3(dot_nn, split(front - back), quarter[2], quarter[3]),
            dot3(dot_nn, split(early - late), odd[0], odd[1]),
        ],
        axis=1,
    )


def cross(left, right):
    out = []
    for base, n in SEGMENTS:
        lr, li = left[:, base : base + n], left[:, base + n : base + 2 * n]
        rr, ri = right[:, base : base + n], right[:, base + n : base + 2 * n]
        out.append(jnp.concatenate([lr * rr + li * ri, li * rr - lr * ri], axis=1))
    return out


def halve_first(x):
    lane = lax.broadcasted_iota(jnp.int32, (1, x.shape[1]), 1)
    return x * jnp.where(lane == 0, 0.5, 1.0).astype(F32)


def unpack(zero, two, rest, quarter, odd):
    p0 = dot3(dot_nt, split(halve_first(zero)), quarter[0], quarter[1])
    p2 = dot3(dot_nt, split(two), quarter[2], quarter[3])
    return p0 + p2, p0 - p2, dot3(dot_nt, split(rest), odd[0], odd[1])


def spread(row):
    return jnp.broadcast_to(row, (LANES, LANES)).T


def columns(index, first):
    rows = [spread(index[first + j : first + j + 1, :]) for j in range(TILE // LANES)]
    return jnp.concatenate(rows, axis=0)


def pairs_kernel(
    count, group, pair_a, pair_b, observed, quarter, odd, corr, remote, local,
    spec, full, conj_terms, plain_terms, target_lags, lags, in_sem, out_sem,
):
    slots = corr.shape[0]
    at = place()
    fetch = pltpu.make_async_copy(observed, target_lags, in_sem)
    fetch.start()
    spectra = spectra_of(lambda c: group[pl.ds(c, QUARTER, stride=8), :], quarter, odd)
    full[...] = spectra
    high, low = split(spectra)
    spec[0:QUARTER, :] = high
    spec[QUARTER:HALF, :] = low
    mine = slot_of(at["core"], at["z"], at["y"]) * 4
    b = pair_b[...]
    placed = ((b >> 2) & 1) * 128 + ((b >> 3) & 7) * 16 + (b >> 6) * 4 + (b & 3)
    live_count = count[...]
    lane = lax.broadcasted_iota(jnp.int32, (TILE, LANES), 1)
    own = [full[pl.ds(mine + q, 1), :] for q in range(4)]
    stores = []

    for i in range(slots // TILE):
        rows = slice(i * TILE, (i + 1) * TILE)
        low_rows = slice(slots + i * TILE, slots + (i + 1) * TILE)
        b_col = columns(placed, i * (TILE // LANES))
        a_col = columns(pair_a, i * (TILE // LANES))
        hot = jnp.concatenate([b_col == lane, b_col == lane + LANES], axis=1).astype(F32).astype(BF16)
        target = dot_nn(hot, spec[0:QUARTER, :]) + dot_nn(hot, spec[QUARTER:HALF, :])
        pieces = []
        for c in range(8):
            row = [jnp.broadcast_to(own[q][:, c * LANES : (c + 1) * LANES], (TILE, LANES)) for q in range(4)]
            pieces.append(
                jnp.where(a_col == 0, row[0], jnp.where(a_col == 1, row[1], jnp.where(a_col == 2, row[2], row[3])))
            )
        source = jnp.concatenate(pieces, axis=1)
        front, back, rest = unpack(*cross(source, target), quarter, odd)
        ahead = (front + rest[:, :QUARTER]) * (2.0 / WIN)
        behind = (back - rest[:, QUARTER:]) * (2.0 / WIN)
        live = lax.broadcasted_iota(jnp.int32, (TILE, QUARTER), 0) + i * TILE < live_count
        lags[rows, 0:QUARTER] = jnp.where(live, behind, 0.0)
        lags[rows, QUARTER:HALF] = jnp.where(live, ahead, 0.0)
        if i == 0:
            fetch.wait()
        res_behind = jnp.where(live, behind - target_lags[rows, 0:QUARTER], 0.0)
        res_ahead = jnp.where(live, ahead - target_lags[rows, QUARTER:HALF], 0.0)
        store = pltpu.make_async_copy(lags.at[rows, :], corr.at[rows, :], out_sem.at[i])
        store.start()
        stores.append(store)
        misfit = (
            dot3(dot_nn, split(res_ahead + res_behind), quarter[0], quarter[1]),
            dot3(dot_nn, split(res_ahead - res_behind), quarter[2], quarter[3]),
            dot3(dot_nn, split(jnp.concatenate([res_ahead, -res_behind], axis=1)), odd[0], odd[1]),
        )
        for (base, n), mis in zip(SEGMENTS, misfit):
            mr, mi = mis[:, :n], mis[:, n:]
            sr, si = source[:, base : base + n], source[:, base + n : base + 2 * n]
            tr, ti = target[:, base : base + n], target[:, base + n : base + 2 * n]
            for terms, re, im in (
                (conj_terms, mr * sr + mi * si, mr * si - mi * sr),
                (plain_terms, mr * tr - mi * ti, mr * ti + mi * tr),
            ):
                for offset, part in ((0, re), (n, im)):
                    part_high, part_low = split(part)
                    cut = slice(base + offset, base + offset + n)
                    terms[rows, cut] = part_high
                    terms[low_rows, cut] = part_low

    def hot_rows(index, height):
        down = lax.broadcasted_iota(jnp.int32, (height, LANES), 0)
        cols = [
            (jnp.broadcast_to(index[i : i + 1, :], (height, LANES)) == down).astype(F32).astype(BF16)
            for i in range(slots // LANES)
        ]
        return jnp.concatenate(cols + cols, axis=1)

    totals = dot_nn(hot_rows(placed, QUARTER), conj_terms[...])
    own_totals = dot_nn(hot_rows(pair_a, 8), plain_terms[...])
    for c in range(8):
        remote[pl.ds(c, QUARTER, stride=8), :] = totals[:, c * LANES : (c + 1) * LANES]
    local[...] = own_totals
    for store in stores:
        store.wait()


def reduce_kernel(
    remote, local, near, quarter_hbm, odd_hbm, lines, plane_in, ring_in, mate_in, sums, total, ends,
    quarter, odd, send_sems, plane_sems, ring_sems, mate_sems, far_sem, table_sems,
):
    at = place()
    y, z, core = at["y"], at["z"], at["core"]
    region = lax.axis_index("region")
    regions = lax.axis_size("region")
    after, before = lax.rem(region + 1, regions), lax.rem(region + regions - 1, regions)
    barrier, count = enter(at)
    pl.semaphore_signal(barrier, inc=1, device_id={"region": before}, device_id_type=MESH)
    fetches = [
        pltpu.make_async_copy(quarter_hbm, quarter, table_sems.at[0]),
        pltpu.make_async_copy(odd_hbm, odd, table_sems.at[1]),
    ]
    for fetch in fetches:
        fetch.start()
    ends[0:32, :] = near[...]
    pl.semaphore_wait(barrier, count + 1)
    send = Sender(send_sems)
    outward = (7, 6, 5, 4, 3, 2, 1, 0)

    def part(cc, zz):
        return pl.ds(pl.multiple_of(slot_of(cc, zz, 0) * 32, 32), NY * 32)

    def block(zz, yy):
        return pl.ds(pl.multiple_of(slot_of(0, zz, yy) * 32, 32), 32)

    def ring(k, d):
        return slice(((k - 1) * NZ + d) * 32, ((k - 1) * NZ + d + 1) * 32)

    def mate(d):
        return slice(d * 32, d * 32 + 32)

    for d in outward:
        zz = flip(z, d)
        send(
            remote.at[part(1 - core, zz), :],
            plane_in.at[part(0, zz), :],
            plane_sems.at[d],
            {"blk": device(y, z, 1 - core)},
        )
    send(near, ends.at[32:64, :], far_sem.at[0], {"region": after})
    for d in outward:
        zz = flip(z, d)
        arrived(plane_in.at[part(0, zz), :], plane_sems.at[d], send_sems, at)
        sums[part(0, zz), :] = remote[part(core, zz), :] + plane_in[part(0, zz), :]
        for k in (2, 1, 3):
            send(
                sums.at[block(zz, turn(y, k)), :],
                ring_in.at[ring(k, d), :],
                ring_sems.at[(k - 1) * NZ + d],
                {"blk": device(turn(y, k), z, core)},
            )
    for d in outward:
        for k in (1, 3, 2):
            arrived(ring_in.at[ring(k, d), :], ring_sems.at[(k - 1) * NZ + d], send_sems, at)
        total[mate(d), :] = (
            sums[block(flip(z, d), y), :] + ring_in[ring(1, d), :] + (ring_in[ring(2, d), :] + ring_in[ring(3, d), :])
        )
        if d:
            send(
                total.at[mate(d), :], mate_in.at[mate(d), :], mate_sems.at[d], {"blk": device(y, flip(z, d), core)}
            )
    for fetch in fetches:
        fetch.wait()
    arrived(ends.at[32:64, :], far_sem.at[0], send_sems, at)
    spectra = spectra_of(lambda c: ends[pl.ds(c, 8, stride=8), :], quarter, odd)
    far = cross(spectra[0:4, :], spectra[4:8, :])
    summed = total[mate(0), :]
    for d in (1, 2, 3, 4, 5, 6, 7):
        arrived(mate_in.at[mate(d), :], mate_sems.at[d], send_sems, at)
        summed = summed + mate_in[mate(d), :]
    total[mate(0), :] = summed

    pieces = [total[pl.ds(c, 4, stride=8), :] for c in range(8)]
    source = jnp.concatenate(pieces, axis=1) + local[0:4, :]
    front, back, rest = unpack(
        *[
            jnp.concatenate([source[:, base : base + 2 * n], far[i]], axis=0)
            for i, (base, n) in enumerate(SEGMENTS)
        ],
        quarter,
        odd,
    )
    plus = (jnp.concatenate([front, back], axis=1) + rest) * (2.0 / WIN)
    minus = (jnp.concatenate([front, back], axis=1) - rest) * (2.0 / WIN)
    lines[:, :HALF] = plus
    lines[:, HALF:] = minus
    send.drain()


def place_kernel(lines, adjoint, far_corr):
    adjoint[...] = lines[0:4, :] * (1.0 / 16.0)
    far_corr[:, :QUARTER] = lines[4:8, WIN - QUARTER :]
    far_corr[:, QUARTER:] = lines[4:8, :QUARTER]


def vmem():
    return pl.BlockSpec(memory_space=pltpu.VMEM)


def smem():
    return pl.BlockSpec(memory_space=pltpu.SMEM)


def anywhere():
    return pl.BlockSpec(memory_space=pl.ANY)


def params(**kw):
    return pltpu.CompilerParams(vmem_limit_bytes=56 * 1024 * 1024, **kw)


def body(records, starts, tapers, pair_a, pair_b, pair_count, observed):
    slots = pair_a.shape[0]
    shape = jax.ShapeDtypeStruct
    quarter, odd = (jnp.asarray(table) for table in tables())
    group, near = pl.pallas_call(
        gather_kernel,
        out_shape=(shape((2048, LANES), F32), shape((32, LANES), F32)),
        in_specs=[smem(), smem(), vmem()],
        out_specs=(vmem(), vmem()),
        scratch_shapes=[
            pltpu.VMEM((64, LANES), F32),
            pltpu.SemaphoreType.DMA((72,)),
            pltpu.SemaphoreType.DMA((64,)),
        ],
        compiler_params=params(collective_id=0, has_side_effects=True),
        name="gather_windows",
    )(starts, tapers, records)
    corr, remote, local = pl.pallas_call(
        pairs_kernel,
        out_shape=(
            shape((slots, HALF), F32),
            shape((2048, LANES), F32),
            shape((8, WIN), F32),
        ),
        in_specs=[vmem()] * 4 + [anywhere()] + [vmem()] * 2,
        out_specs=(anywhere(), vmem(), vmem()),
        scratch_shapes=[
            pltpu.VMEM((HALF, WIN), BF16),
            pltpu.VMEM((QUARTER, WIN), F32),
            pltpu.VMEM((2 * slots, WIN), BF16),
            pltpu.VMEM((2 * slots, WIN), BF16),
            pltpu.VMEM((slots, HALF), F32),
            pltpu.VMEM((slots, HALF), F32),
            pltpu.SemaphoreType.DMA,
            pltpu.SemaphoreType.DMA((slots // TILE,)),
        ],
        compiler_params=params(),
        name="pairs",
    )(
        pair_count.reshape(1, 1),
        group,
        pair_a.reshape(slots // LANES, LANES),
        pair_b.reshape(slots // LANES, LANES),
        observed,
        quarter,
        odd,
    )
    lines = pl.pallas_call(
        reduce_kernel,
        out_shape=shape((8, WIN), F32),
        in_specs=[vmem()] * 3 + [anywhere()] * 2,
        out_specs=vmem(),
        scratch_shapes=[
            pltpu.VMEM((1024, LANES), F32),
            pltpu.VMEM((768, LANES), F32),
            pltpu.VMEM((256, LANES), F32),
            pltpu.VMEM((1024, LANES), F32),
            pltpu.VMEM((256, LANES), F32),
            pltpu.VMEM((64, LANES), F32),
            pltpu.VMEM(quarter.shape, BF16),
            pltpu.VMEM(odd.shape, BF16),
            pltpu.SemaphoreType.DMA((40,)),
            pltpu.SemaphoreType.DMA((8,)),
            pltpu.SemaphoreType.DMA((24,)),
            pltpu.SemaphoreType.DMA((8,)),
            pltpu.SemaphoreType.DMA((1,)),
            pltpu.SemaphoreType.DMA((2,)),
        ],
        compiler_params=params(collective_id=1, has_side_effects=True),
        name="reduce_terms",
    )(remote, local, near, quarter, odd)
    adjoint, far_corr = pl.pallas_call(
        place_kernel,
        out_shape=(shape((4, WIN), F32), shape((4, HALF), F32)),
        in_specs=[vmem()],
        out_specs=(vmem(), vmem()),
        compiler_params=params(),
        name="place_lines",
    )(lines)
    return corr, far_corr, adjoint


def solution(mesh):
    split_all = P(("region", "blk"))
    rows = P(("region", "blk"), None)
    return jax.shard_map(
        body,
        mesh=mesh,
        in_specs=(rows, split_all, split_all, split_all, split_all, split_all, rows),
        out_specs=(rows, rows, rows),
        check_vma=False,
    )
```
